32 devices in a mesh: ctx: 8 (over z, x), head: 4 (over y, core).
Axes of the slice: x: 2, y: 2, z: 4, core: 2. Of those that a mesh axis runs over, the one named last changes fastest.
Arguments:
- x_in: bfloat16 [8192, 4096], P('ctx', 'head'), may hold values from -6 to 6
- b_in: bfloat16 [8192, 128], P('ctx'), may hold values from -1.796875 to 1.796875
- c_in: bfloat16 [8192, 128], P('ctx'), may hold values from -1.796875 to 1.796875
- d_out: bfloat16 [8192, 4096], P('ctx', 'head'), may hold values from -0.75 to 0.75
- table: float32 [16, 18], replicated, may hold values from 0 to 3, as said below
- level_index: int32 [8192], P('ctx'), may hold values from 0 to 15
Outputs:
- y_out: bfloat16 [8192, 4096], P('ctx', 'head')
- dx_out: bfloat16 [8192, 4096], P('ctx', 'head')
- d_b: float32 [8192, 128], P(('ctx', 'head'))
- d_c: float32 [8192, 128], P(('ctx', 'head'))
The draws below stay inside these ranges and needn't reach their ends.
Inputs may be any that keep to these rules, and one draw needn't show every extreme that they name: `table`: entries are positive.
All inputs are finite; a program needn't handle non-finite values.
Results may differ from the reference program's by a relative error of at most 0.006.
Values sent between devices are 32-bit elements; how exact they have to be, the bound alone decides.
A program may use at most 128 MiB of HBM per device.

```python
import jax
import jax.numpy as jnp
from jax import lax

HEADS = 64
HEAD_DIM = 64
NSTATE = 128
TOK_DEV = 1024
NTAB = 16
LEVELS = 18
TOKENS = 8192
WIDTH = 4096
N_CTX = 8
N_HEAD = 4


def draw_table(key, part):
    raw_draw = jax.random.uniform(key, (NTAB, LEVELS), jnp.float32)
    row_scale = jnp.exp(jnp.log(0.3) + raw_draw * jnp.log(10.0))
    falloff = jnp.exp2(-0.5 * jnp.arange(LEVELS, dtype=jnp.float32))
    return (row_scale * falloff[None, :]).astype(jnp.float32)


def set_ends(values, stream_key, smallest, high):
    longest = values.shape.index(max(values.shape))
    spots = []
    for shift in (0, 1):
        where = [jax.random.randint(jax.random.fold_in(stream_key, axis), (), 0, length) for axis, length in enumerate(values.shape)]
        where[longest] = (where[longest] + shift) % values.shape[longest]
        spots.append(tuple(where))
    return values.at[spots[0]].set(smallest).at[spots[1]].set(high)


def block_scale(rng, extent, split, low, high):
    loudness = 1.0
    for dim, shards_of in split:
        draws = jax.random.uniform(jax.random.fold_in(jax.random.fold_in(rng, 6), dim), (shards_of,), jnp.float32, low / len(split), high / len(split))
        loudness = loudness * jnp.repeat(jnp.exp(draws), extent[dim] // shards_of).reshape((-1,) + (1,) * (len(extent) - 1 - dim))
    return loudness


def normal_values(rng, extent, width, most, cuts=(), kind=jnp.bfloat16):
    loudness = block_scale(rng, extent, cuts, -0.22, 0.18) if cuts else 1.0
    values = jax.random.normal(rng, extent, jnp.float32) * width * loudness
    return jnp.minimum(jnp.maximum(values, -most), most).astype(kind)


def setup_inputs(seed: int = 0) -> dict:
    key_of = jax.random.split(jax.random.key(seed), 7)
    x_in = normal_values(key_of[0], (TOKENS, WIDTH), 1.0, 6.0, ((0, 8), (1, 4)))
    b_in = normal_values(key_of[1], (TOKENS, NSTATE), 0.3, 1.796875, ((0, 8),))
    c_in = normal_values(key_of[2], (TOKENS, NSTATE), 0.3, 1.796875, ((0, 8),))
    d_out = normal_values(key_of[3], (TOKENS, WIDTH), 0.125, 0.75, ((0, 8), (1, 4)))
    table = draw_table(jax.random.fold_in(key_of[6], 71), 0)
    level_index = set_ends(jax.random.randint(key_of[5], (TOKENS,), 0, NTAB), jax.random.fold_in(key_of[5], 1), 0, NTAB - 1).astype(jnp.int32)
    return dict(x_in=x_in, b_in=b_in, c_in=c_in, d_out=d_out, table=table, level_index=level_index)


def bit_count(values, bits):
    counted = jnp.zeros(values.shape, jnp.int32)
    for digit_no in range(bits):
        counted = counted + (values >= (1 << digit_no)).astype(jnp.int32)
    return counted


def reference(x_in, b_in, c_in, d_out, table, level_index):
    num_blocks = N_CTX
    tok_rows = TOK_DEV
    feat_width = HEADS * HEAD_DIM
    groups_head = N_HEAD
    ctx_bits = num_blocks.bit_length() - 1
    low_bits = tok_rows.bit_length() - 1
    weights_tok = table[level_index]
    xs_block = x_in.reshape(num_blocks, tok_rows, feat_width)
    bs_block = b_in.reshape(num_blocks, tok_rows, NSTATE)
    cs_block = c_in.reshape(num_blocks, tok_rows, NSTATE)
    ds_block = d_out.reshape(num_blocks, tok_rows, feat_width)
    lam_block = weights_tok.reshape(num_blocks, tok_rows, LEVELS)
    state = jnp.einsum("cln,clp->cnp", bs_block.astype(jnp.float32), xs_block.astype(jnp.float32))
    block_ids = jnp.arange(num_blocks, dtype=jnp.int32)
    top_bit = bit_count(block_ids[:, None] ^ block_ids[None, :], ctx_bits) - 1
    level_ids = jnp.arange(ctx_bits, dtype=jnp.int32)
    same_level = top_bit[:, None, :] == level_ids[None, :, None]
    below = (same_level & (block_ids[None, None, :] < block_ids[:, None, None])).astype(jnp.float32)
    above = (same_level & (block_ids[None, None, :] > block_ids[:, None, None])).astype(jnp.float32)
    carry = jnp.einsum("cke,enp->cknp", below, state, precision=lax.Precision.HIGHEST).astype(jnp.bfloat16)
    far_lam = lam_block[:, :, low_bits + 1:low_bits + 1 + ctx_bits]
    rising = (far_lam[:, :, :, None] * cs_block[:, :, None, :].astype(jnp.float32)).astype(jnp.bfloat16)
    grad_state = jnp.einsum("clkn,clp->cknp", rising.astype(jnp.float32), ds_block.astype(jnp.float32))
    back_state = jnp.einsum("cke,eknp->cnp", above, grad_state, precision=lax.Precision.HIGHEST).astype(jnp.bfloat16)
    positions = jnp.arange(tok_rows, dtype=jnp.int32)
    local_level = bit_count(positions[:, None] ^ positions[None, :], low_bits)
    causal = positions[None, :] <= positions[:, None]

    def one_block(bundle):
        x_blk, b_blk, c_blk, d_blk, lam_blk, carry_blk, rise_blk, back_blk = bundle
        weight = jnp.take_along_axis(lam_blk, local_level, axis=1)
        weight = jnp.where(causal, weight, 0.0)
        scores = jnp.dot(c_blk, b_blk.T, preferred_element_type=jnp.float32)
        mixing = (scores * weight).astype(jnp.bfloat16)
        flat_carry = carry_blk.reshape(ctx_bits * NSTATE, feat_width)
        flat_rise = rise_blk.reshape(tok_rows, ctx_bits * NSTATE)
        y_blk = jnp.dot(mixing, x_blk, preferred_element_type=jnp.float32) + jnp.dot(flat_rise, flat_carry, preferred_element_type=jnp.float32)
        dx_blk = jnp.dot(mixing.T, d_blk, preferred_element_type=jnp.float32) + jnp.dot(b_blk, back_blk, preferred_element_type=jnp.float32)
        per_group = jnp.einsum("lgp,mgp->glm", d_blk.reshape(tok_rows, groups_head, -1).astype(jnp.float32), x_blk.reshape(tok_rows, groups_head, -1).astype(jnp.float32))
        d_mix = (per_group * weight[None]).astype(jnp.bfloat16).astype(jnp.float32)
        grad_c = jnp.einsum("glm,mn->ln", d_mix, b_blk.astype(jnp.float32))
        grad_b = jnp.einsum("glm,ln->mn", d_mix, c_blk.astype(jnp.float32))
        far_terms = jnp.dot(d_blk, flat_carry.T, preferred_element_type=jnp.float32).reshape(tok_rows, ctx_bits, NSTATE)
        grad_c = grad_c + jnp.sum(far_terms * lam_blk[:, low_bits + 1:low_bits + 1 + ctx_bits, None], axis=1)
        grad_b = grad_b + jnp.dot(x_blk, back_blk.T, preferred_element_type=jnp.float32)
        return y_blk.astype(jnp.bfloat16), dx_blk.astype(jnp.bfloat16), grad_b, grad_c

    y_all, dx_all, gb_all, gc_all = lax.map(one_block, (xs_block, bs_block, cs_block, ds_block, lam_block, carry, rising, back_state))
    total_rows = num_blocks * tok_rows
    return (y_all.reshape(total_rows, feat_width), dx_all.reshape(total_rows, feat_width), gb_all.reshape(total_rows, NSTATE), gc_all.reshape(total_rows, NSTATE))
```

```python
import jax
import jax.numpy as jnp
from jax import lax
from jax.sharding import PartitionSpec as P

CHUNKS = 2


def f32_dot(a, b):
    return jnp.dot(a, b, preferred_element_type=jnp.float32)


def bit_count(values, bits):
    counted = jnp.zeros(values.shape, jnp.int32)
    for digit_no in range(bits):
        counted = counted + (values >= 1 << digit_no).astype(jnp.int32)
    return counted


def level_routes(count, bits):
    routes = []
    for k in range(bits):
        if k == 0:
            routes.append([[(low, low + 1) for low in range(0, count, 2)]])
            continue
        top = (1 << k) - 2
        hops = []
        for step in range(1 << (k - 1)):
            hops.append(
                [
                    (base + top + par, base + (1 << k) + 2 * step + par)
                    for base in range(0, count, 2 << k)
                    for par in (0, 1)
                ]
            )
        routes.append(hops)
    return routes


def carries(state, routes):
    both = routes[0][0] + [(high, low) for low, high in routes[0][0]]
    other = lax.ppermute(state, "ctx", both)
    upper = (lax.axis_index("ctx") & 1).astype(jnp.float32)
    parts = [other * upper]
    group = state + other
    for hops in routes[1:]:
        got = sum(lax.ppermute(group, "ctx", hop) for hop in hops)
        parts.append(got)
        group = group + got
    return jnp.concatenate(parts, axis=0).astype(jnp.bfloat16)


def local(x_in, b_in, c_in, d_out, table, level_index):
    tok_rows, feat_width = x_in.shape
    nstate = b_in.shape[1]
    low_bits = tok_rows.bit_length() - 1
    count = lax.axis_size("ctx")
    ctx_bits = count.bit_length() - 1
    my_block = lax.axis_index("ctx")
    parity = my_block & 1
    table_rows = table.shape[0]
    chooser = (level_index[:, None] == jnp.arange(table_rows, dtype=jnp.int32)[None, :]).astype(
        jnp.float32
    )
    weights_tok = jnp.dot(chooser, table, precision=lax.Precision.HIGHEST)
    far_lam = weights_tok[:, low_bits + 1 : low_bits + 1 + ctx_bits]
    rising = (
        (far_lam[:, :, None] * c_in[:, None, :].astype(jnp.float32))
        .astype(jnp.bfloat16)
        .reshape(tok_rows, ctx_bits * nstate)
    )
    routes = level_routes(count, ctx_bits)
    both = routes[0][0] + [(high, low) for low, high in routes[0][0]]
    step = feat_width // CHUNKS
    carry_chunks, back_chunks = [], []
    for start in range(0, feat_width, step):
        xs = x_in[:, start : start + step]
        ds = d_out[:, start : start + step]
        carry_chunks.append(carries(f32_dot(b_in.T, xs), routes))
        grads = f32_dot(rising.T, ds).reshape(ctx_bits, nstate, step)
        total = jnp.zeros((nstate, step), jnp.float32)
        for k in range(ctx_bits - 1, 0, -1):
            got = jnp.zeros((nstate, step), jnp.float32)
            for hop_no, hop in enumerate(routes[k]):
                down = [(high, low) for low, high in hop]
                sent = grads[k] + total if hop_no == len(routes[k]) - 1 else grads[k]
                got = got + lax.ppermute(sent, "ctx", down)
            total = total + got
        odd = parity.astype(jnp.float32)
        other = lax.ppermute(total + grads[0] * odd, "ctx", both)
        back_chunks.append((total + other).astype(jnp.bfloat16))
    carry = jnp.concatenate(carry_chunks, axis=1)
    back_state = jnp.concatenate(back_chunks, axis=1)
    positions = jnp.arange(tok_rows, dtype=jnp.int32)
    y_parts = []
    c_parts = []
    dx_accum = jnp.zeros((tok_rows, feat_width), jnp.float32)
    grad_b = jnp.zeros((tok_rows, nstate), jnp.float32)
    block_rows = min(512, tok_rows)
    for row_start in range(0, tok_rows, block_rows):
        row_stop = row_start + block_rows
        row_pos = positions[row_start:row_stop]
        col_pos = positions[:row_stop]
        level_map = bit_count(row_pos[:, None] ^ col_pos[None, :], low_bits)
        weight = jnp.zeros((block_rows, row_stop), jnp.float32)
        for level_no in range(low_bits + 1):
            weight = weight + jnp.where(
                level_map == level_no, weights_tok[row_start:row_stop, level_no][:, None], 0.0
            )
        weight = jnp.where(col_pos[None, :] <= row_pos[:, None], weight, 0.0)
        scores = f32_dot(c_in[row_start:row_stop], b_in[:row_stop].T)
        mixing = (scores * weight).astype(jnp.bfloat16)
        y_parts.append(f32_dot(mixing, x_in[:row_stop]))
        dx_accum = dx_accum.at[:row_stop].add(f32_dot(mixing.T, d_out[row_start:row_stop]))
        d_mix = (f32_dot(d_out[row_start:row_stop], x_in[:row_stop].T) * weight).astype(
            jnp.bfloat16
        )
        c_parts.append(f32_dot(d_mix, b_in[:row_stop]))
        grad_b = grad_b.at[:row_stop].add(f32_dot(d_mix.T, c_in[row_start:row_stop]))
    y_near = jnp.concatenate(y_parts, axis=0)
    grad_c = jnp.concatenate(c_parts, axis=0)
    far_terms = f32_dot(d_out, carry.T).reshape(tok_rows, ctx_bits, nstate)
    grad_c = grad_c + jnp.sum(far_terms * far_lam[:, :, None], axis=1)
    grad_b = grad_b + f32_dot(x_in, back_state.T)
    heads = lax.axis_size("head")
    head_bits = heads.bit_length() - 1
    my_head = lax.axis_index("head")
    rows = tok_rows // heads
    pair = jnp.stack([grad_b, grad_c]).reshape(2, heads, rows, nstate)
    for digit_no in range(head_bits):
        mine = my_head >> digit_no & 1
        pair = pair.reshape(2, pair.shape[1] // 2, 2, rows, nstate)
        keep = jnp.where(mine == 1, pair[:, :, 1], pair[:, :, 0])
        sent = jnp.where(mine == 1, pair[:, :, 0], pair[:, :, 1])
        swap = [(h, h ^ (1 << digit_no)) for h in range(heads)]
        pair = keep + lax.ppermute(sent, "head", swap)
    y_out = (y_near + f32_dot(rising, carry)).astype(jnp.bfloat16)
    dx_out = (dx_accum + f32_dot(b_in, back_state)).astype(jnp.bfloat16)
    pair = pair.reshape(2, rows, nstate)
    return (y_out, dx_out, pair[0], pair[1])


def solution(mesh):
    return jax.shard_map(
        local,
        mesh=mesh,
        in_specs=(
            P("ctx", "head"),
            P("ctx", None),
            P("ctx", None),
            P("ctx", "head"),
            P(),
            P("ctx"),
        ),
        out_specs=(
            P("ctx", "head"),
            P("ctx", "head"),
            P(("ctx", "head"), None),
            P(("ctx", "head"), None),
        ),
        check_vma=False,
    )
```

```python
import functools

import jax
import jax.numpy as jnp
from jax import lax
from jax.experimental import pallas as pl
from jax.experimental.pallas import tpu as pltpu
from jax.sharding import PartitionSpec as P

F32 = jnp.float32
BF16 = jnp.bfloat16
MESH = pl.DeviceIdType.MESH
TILE = 256
WIDTH = 256


def mm(a, b):
    return jnp.dot(a, b, preferred_element_type=F32)


def mm_tn(a, b):
    return lax.dot_general(a, b, (((0,), (0,)), ((), ())), preferred_element_type=F32)


def mm_nt(a, b):
    return lax.dot_general(a, b, (((1,), (1,)), ((), ())), preferred_element_type=F32)


def bit_count(values, bits):
    counted = jnp.zeros(values.shape, jnp.int32)
    for digit_no in range(bits):
        counted = counted + (values >= 1 << digit_no).astype(jnp.int32)
    return counted


def kernel(
    count,
    heads,
    x_ref,
    b_ref,
    c_ref,
    d_ref,
    w_ref,
    far_t_ref,
    y_ref,
    dx_ref,
    db_ref,
    dc_ref,
    y_acc,
    dx_acc,
    grads,
    rise,
    rise_t,
    carry,
    s_buf,
    g_buf,
    rx0,
    up,
    rc,
    rb,
    tot,
    xb,
    rxb,
    *rest,
):
    bits = count.bit_length() - 1
    head_bits = heads.bit_length() - 1
    r_in = rest[:head_bits]
    r_out = rest[head_bits : 2 * head_bits - 1]
    sems = rest[2 * head_bits - 1 :]
    (x0_s, x0_r, up_s, rc_r, bk_s, rb_r, xb_s, xb_r), hd_sems = sems[:8], sems[8:]
    toks, feats = x_ref.shape
    nstate = b_ref.shape[1]
    chunks = feats // WIDTH
    blocks = toks // TILE
    tile_bits = TILE.bit_length() - 1
    low_bits = toks.bit_length() - 1
    me = lax.axis_index("ctx")
    head = lax.axis_index("head")
    par = me % 2
    col = me // 2
    levels = range(1, bits)
    top = {k: col % (1 << k) == (1 << (k - 1)) - 1 for k in levels}
    is_set = {k: (me // (1 << k)) % 2 == 1 for k in range(bits)}
    last = col == count // 2 - 1
    late = {
        k: is_set[k] & ((col % (1 << k) != (1 << k) - 1) | last) for k in levels
    }

    barrier = pltpu.get_barrier_semaphore()
    for off in range(1, count):
        pl.semaphore_signal(
            barrier, inc=1, device_id={"ctx": (me + off) % count}, device_id_type=MESH
        )
    for off in range(1, heads):
        pl.semaphore_signal(
            barrier, inc=1, device_id={"head": (head + off) % heads}, device_id_type=MESH
        )

    def remote(src, dst, ssem, rsem, device):
        return pltpu.make_async_remote_copy(
            src_ref=src,
            dst_ref=dst,
            send_sem=ssem,
            recv_sem=rsem,
            device_id=device,
            device_id_type=MESH,
        )

    partner = me + 1 - 2 * par

    def x0_copy(q):
        return remote(s_buf.at[q], rx0.at[q], x0_s.at[q], x0_r.at[q], {"ctx": partner})

    def up_copy(k, step, q):
        return remote(
            up.at[q],
            rc.at[k - 1, q],
            up_s.at[step, q],
            rc_r.at[k - 1, q],
            {"ctx": (me + 2 + 2 * step) % count},
        )

    def back_copy(k, q):
        step = (me % (1 << k)) // 2
        dest = (me // (2 << k)) * (2 << k) + (1 << k) - 2 + par
        return remote(
            g_buf.at[k, q], rb.at[step, q], bk_s.at[k - 1, q], rb_r.at[step, q], {"ctx": dest}
        )

    def rb_wait(step, q):
        remote(
            g_buf.at[0, q], rb.at[step, q], bk_s.at[0, q], rb_r.at[step, q], {"ctx": partner}
        ).wait_recv()

    def xb_copy(q):
        return remote(xb.at[q], rxb.at[q], xb_s.at[q], xb_r.at[q], {"ctx": partner})

    b_t = b_ref[...].astype(F32).T.astype(BF16)
    c_f = c_ref[...].astype(F32)
    c_t = c_f.T
    for k in range(bits):
        rise_t[k * nstate : (k + 1) * nstate, :] = (c_t * far_t_ref[k : k + 1, :]).astype(BF16)
        lam = w_ref[:, low_bits + 1 + k : low_bits + 2 + k]
        rise[:, k * nstate : (k + 1) * nstate] = (c_f * lam).astype(BF16)
    pl.semaphore_wait(barrier, count - 1 + heads - 1)
    for q in range(chunks):
        cols = slice(q * WIDTH, (q + 1) * WIDTH)
        s_buf[q] = mm(b_t, x_ref[:, cols])
        x0_copy(q).start()
    for q in range(chunks):
        cols = slice(q * WIDTH, (q + 1) * WIDTH)
        g_buf[:, q] = mm(rise_t[...], d_ref[:, cols]).reshape(bits, nstate, WIDTH)
        if bits > 1:

            @pl.when(late[bits - 1])
            def _():
                back_copy(bits - 1, q).start()

    for k in reversed(range(1, bits - 1)):
        for q in range(chunks):

            @pl.when(late[k])
            def _():
                back_copy(k, q).start()

    def tile(i, j, diagonal):
        rows = pl.ds(i * TILE, TILE)
        cols = pl.ds(pl.multiple_of(j * TILE, TILE), TILE)
        w_rows = w_ref[rows, :]
        if diagonal:
            row = lax.broadcasted_iota(jnp.int32, (TILE, TILE), 0)
            at = lax.broadcasted_iota(jnp.int32, (TILE, TILE), 1)
            level = bit_count(row ^ at, tile_bits)
            weight = jnp.zeros((TILE, TILE), F32)
            for n in range(tile_bits + 1):
                weight = jnp.where(level == n, w_rows[:, n : n + 1], weight)
            weight = jnp.where(at <= row, weight, 0.0)
        else:
            far = i ^ j
            level = tile_bits
            for n in range(blocks.bit_length() - 1):
                level = level + (far >= 1 << n).astype(jnp.int32)
            lane = lax.broadcasted_iota(jnp.int32, w_rows.shape, 1)
            weight = jnp.sum(jnp.where(lane == level, w_rows, 0.0), axis=1, keepdims=True)
        x_j, d_i, b_j, c_i = x_ref[cols, :], d_ref[rows, :], b_ref[cols, :], c_ref[rows, :]
        mix = (mm_nt(c_i, b_j) * weight).astype(BF16)
        d_mix = (mm_nt(d_i, x_j) * weight).astype(BF16)
        y_t, dx_t = mm(mix, x_j), mm_tn(mix, d_i)
        dc_t, db_t = mm(d_mix, b_j), mm_tn(d_mix, c_i)
        if diagonal:
            y_acc[rows, :] = y_t
            dx_acc[cols, :] = dx_t
            grads[1, rows, :] = dc_t
            grads[0, cols, :] = db_t
        else:
            y_acc[rows, :] += y_t
            dx_acc[cols, :] += dx_t
            grads[1, rows, :] += dc_t
            grads[0, cols, :] += db_t

    def near(i):
        tile(i, i, True)
        if i:

            def step(j, none):
                tile(i, j, False)
                return none

            lax.fori_loop(0, i, step, 0)

    def pass_up(q):
        x0_copy(q).wait_recv()
        for k in levels:

            @pl.when(top[k])
            def _():
                group = s_buf[q] + rx0[q]
                for j in range(1, k):
                    up_copy(j, 0, q).wait_recv()
                    group = group + rc[j - 1, q]
                up[q] = group
                for step in range(1 << (k - 1)):
                    up_copy(k, step, q).start()

    def pass_down(q):
        if bits > 1:

            @pl.when(last)
            def _():
                tot[q] = jnp.zeros_like(tot[q])
        else:
            tot[q] = jnp.zeros_like(tot[q])

        for k in levels:

            @pl.when(top[k])
            def _():
                for step in range(1 << (k - 1)):
                    rb_wait(step, q)
                got = rb[0, q]
                for step in range(1, 1 << (k - 1)):
                    got = got + rb[step, q]
                tot[q] = got
                for j in range(1, k):
                    g_buf[j, q] = g_buf[j, q] + got
                    back_copy(j, q).start()

        @pl.when(par == 1)
        def _():
            xb[q] = tot[q] + g_buf[0, q]

        @pl.when(par == 0)
        def _():
            xb[q] = tot[q]

        xb_copy(q).start()

    def far(q):
        cols = slice(q * WIDTH, (q + 1) * WIDTH)
        for k in range(bits):
            at = slice(k * nstate, (k + 1) * nstate)
            if k:

                @pl.when(late[k])
                def _():
                    up_copy(k, 0, q).wait_recv()

            @pl.when(is_set[k])
            def _():
                carry[at, :] = (rc[k - 1, q] if k else rx0[q]).astype(BF16)

            @pl.when(jnp.logical_not(is_set[k]))
            def _():
                carry[at, :] = jnp.zeros((nstate, WIDTH), BF16)

        y_ref[:, cols] = (y_acc[:, cols] + mm(rise[...], carry[...])).astype(BF16)
        for i in range(blocks):
            rows = slice(i * TILE, (i + 1) * TILE)
            terms = mm_nt(d_ref[rows, cols], carry[...])
            total = grads[1, rows, :]
            for k in range(bits):
                lam = w_ref[rows, low_bits + 1 + k : low_bits + 2 + k]
                total = total + terms[:, k * nstate : (k + 1) * nstate] * lam
            grads[1, rows, :] = total
        xb_copy(q).wait_recv()
        back = (tot[q] + rxb[q]).astype(BF16)
        dx_ref[:, cols] = (dx_acc[:, cols] + mm(b_ref[...], back)).astype(BF16)
        grads[0] = grads[0] + mm_nt(x_ref[:, cols], back)

    for n in range(max(chunks, blocks)):
        if n < chunks:
            pass_up(n)
        if n < blocks:
            near(n)
    for n in range(chunks + 1):
        if n < chunks:
            pass_down(n)
        if n:
            far(n - 1)

    rows = toks // heads
    now, waits = [], []
    pieces = heads
    for digit in range(head_bits):
        pieces //= 2
        mine = (head // (1 << digit)) % 2
        peer = head + (1 - 2 * mine) * (1 << digit)
        ssem, rsem = hd_sems[2 * digit], hd_sems[2 * digit + 1]

        def piece(array, g, which):
            if digit == 0:
                start = pl.multiple_of((2 * g + which) * rows, rows)
                return grads.at[array, pl.ds(start, rows)]
            return r_out[digit - 1].at[array, 2 * g + which]

        copies = {}
        for array in range(2):
            for g in range(pieces):
                copies[array, g] = remote(
                    piece(array, g, 1 - mine),
                    r_in[digit].at[array, g],
                    ssem.at[array, g],
                    rsem.at[array, g],
                    {"head": peer},
                )
                copies[array, g].start()
        for array in range(2):
            for g in range(pieces):
                copies[array, g].wait_recv()
                value = piece(array, g, mine)[...] + r_in[digit][array, g]
                if digit < head_bits - 1:
                    r_out[digit][array, g] = value
                else:
                    (db_ref, dc_ref)[array][...] = value
        waits += list(copies.values())
    if not head_bits:
        db_ref[...] = grads[0]
        dc_ref[...] = grads[1]

    for copy in waits:
        copy.wait_send()
    for q in range(chunks):
        x0_copy(q).wait_send()
        xb_copy(q).wait_send()
        for k in levels:

            @pl.when(top[k])
            def _():
                for step in range(1 << (k - 1)):
                    up_copy(k, step, q).wait_send()

            @pl.when(is_set[k])
            def _():
                back_copy(k, q).wait_send()


def local(x_in, b_in, c_in, d_out, table, level_index):
    toks, feats = x_in.shape
    nstate = b_in.shape[1]
    count, heads = lax.axis_size("ctx"), lax.axis_size("head")
    bits, head_bits = count.bit_length() - 1, heads.bit_length() - 1
    low_bits = toks.bit_length() - 1
    chunks = feats // WIDTH
    chooser = (
        level_index[:, None] == jnp.arange(table.shape[0], dtype=jnp.int32)[None, :]
    ).astype(F32)
    w_tok = jnp.dot(chooser, table, precision=lax.Precision.HIGHEST)
    far_t = w_tok[:, low_bits + 1 : low_bits + 1 + bits].T
    rows = toks // heads
    fan = 1 << max(bits - 2, 0)
    ups = max(bits - 1, 1)
    vmem = pl.BlockSpec(memory_space=pltpu.VMEM)
    dma = pltpu.SemaphoreType.DMA
    slab = (chunks, nstate, WIDTH)
    halves = [heads >> (n + 1) for n in range(head_bits)]
    return pl.pallas_call(
        functools.partial(kernel, count, heads),
        out_shape=(
            jax.ShapeDtypeStruct((toks, feats), BF16),
            jax.ShapeDtypeStruct((toks, feats), BF16),
            jax.ShapeDtypeStruct((rows, nstate), F32),
            jax.ShapeDtypeStruct((rows, nstate), F32),
        ),
        in_specs=[vmem] * 6,
        out_specs=(vmem,) * 4,
        scratch_shapes=[
            pltpu.VMEM((toks, feats), F32),
            pltpu.VMEM((toks, feats), F32),
            pltpu.VMEM((2, toks, nstate), F32),
            pltpu.VMEM((toks, bits * nstate), BF16),
            pltpu.VMEM((bits * nstate, toks), BF16),
            pltpu.VMEM((bits * nstate, WIDTH), BF16),
            pltpu.VMEM(slab, F32),
            pltpu.VMEM((bits,) + slab, F32),
            pltpu.VMEM(slab, F32),
            pltpu.VMEM(slab, F32),
            pltpu.VMEM((ups,) + slab, F32),
            pltpu.VMEM((fan,) + slab, F32),
            pltpu.VMEM(slab, F32),
            pltpu.VMEM(slab, F32),
            pltpu.VMEM(slab, F32),
        ]
        + [pltpu.VMEM((2, half, rows, nstate), F32) for half in halves]
        + [pltpu.VMEM((2, half, rows, nstate), F32) for half in halves[:-1]]
        + [
            dma((chunks,)),
            dma((chunks,)),
            dma((fan, chunks)),
            dma((ups, chunks)),
            dma((ups, chunks)),
            dma((fan, chunks)),
            dma((chunks,)),
            dma((chunks,)),
        ]
        + [dma((2, half)) for half in halves for _ in range(2)],
        compiler_params=pltpu.CompilerParams(
            collective_id=0, has_side_effects=True, vmem_limit_bytes=60 * 1024 * 1024
        ),
    )(x_in, b_in, c_in, d_out, w_tok, far_t)


def solution(mesh):
    return jax.shard_map(
        local,
        mesh=mesh,
        in_specs=(
            P("ctx", "head"),
            P("ctx", None),
            P("ctx", None),
            P("ctx", "head"),
            P(),
            P("ctx"),
        ),
        out_specs=(
            P("ctx", "head"),
            P("ctx", "head"),
            P(("ctx", "head"), None),
            P(("ctx", "head"), None),
        ),
        check_vma=False,
    )
```

```python
import functools

import jax
import jax.numpy as jnp
from jax import lax
from jax.experimental import pallas as pl
from jax.experimental.pallas import tpu as pltpu
from jax.sharding import PartitionSpec as P

F32 = jnp.float32
BF16 = jnp.bfloat16
MESH = pl.DeviceIdType.MESH
TILE = 256
WIDTH = 256


def mm(a, b):
    return jnp.dot(a, b, preferred_element_type=F32)


def mm_tn(a, b):
    return lax.dot_general(a, b, (((0,), (0,)), ((), ())), preferred_element_type=F32)


def mm_nt(a, b):
    return lax.dot_general(a, b, (((1,), (1,)), ((), ())), preferred_element_type=F32)


def bit_count(values, bits):
    counted = jnp.zeros(values.shape, jnp.int32)
    for digit_no in range(bits):
        counted = counted + (values >= 1 << digit_no).astype(jnp.int32)
    return counted


def kernel(
    count,
    heads,
    x_hbm,
    b_ref,
    c_ref,
    d_hbm,
    table_ref,
    index_ref,
    y_ref,
    dx_ref,
    db_ref,
    dc_ref,
    x_ref,
    d_ref,
    w_ref,
    y_acc,
    dx_acc,
    grads,
    rise,
    rise_t,
    carry,
    s_buf,
    g_buf,
    rx0,
    up,
    rc,
    rb,
    tot,
    xb,
    rxb,
    *rest,
):
    bits = count.bit_length() - 1
    head_bits = heads.bit_length() - 1
    r_in = rest[:head_bits]
    r_out = rest[head_bits : 2 * head_bits - 1]
    sems = rest[2 * head_bits - 1 :]
    in_sem, x0_s, x0_r, up_s, fw_s, rc_r, bk_s, rb_r, xb_s, xb_r = sems[:10]
    hd_sems = sems[10:]
    toks, feats = x_ref.shape
    nstate = b_ref.shape[1]
    chunks = feats // WIDTH
    blocks = toks // TILE
    tile_bits = TILE.bit_length() - 1
    low_bits = toks.bit_length() - 1
    me = lax.axis_index("ctx")
    head = lax.axis_index("head")
    par = me % 2
    col = me // 2
    levels = range(1, bits)
    columns = count // 2
    is_set = {k: (me // (1 << k)) % 2 == 1 for k in range(bits)}
    low_top = {k: col % (1 << k) == (1 << (k - 1)) - 1 for k in levels}
    up_top = {k: col % (1 << k) == (1 << k) - 1 for k in levels}
    relay = {k: is_set[k] & jnp.logical_not(up_top[k]) for k in levels}
    last = col == columns - 1
    ready = {k: up_top[k] & last for k in levels}
    early = {k: up_top[k] & jnp.logical_not(last) for k in levels}
    late = {k: up_top[k] & last for k in levels}

    def fill(hbm, vmem, n, q):
        cols = pl.ds(q * WIDTH, WIDTH)
        return pltpu.make_async_copy(hbm.at[:, cols], vmem.at[:, cols], in_sem.at[n, q])

    for q in range(chunks):
        fill(x_hbm, x_ref, 0, q).start()
    for q in range(chunks):
        fill(d_hbm, d_ref, 1, q).start()

    partner = me + 1 - 2 * par
    barrier = pltpu.get_barrier_semaphore()
    pl.semaphore_signal(barrier, inc=1, device_id={"ctx": partner}, device_id_type=MESH)
    for digit in range(head_bits):
        flip = 1 - 2 * ((head // (1 << digit)) % 2)
        pl.semaphore_signal(
            barrier, inc=1, device_id={"head": head + flip * (1 << digit)}, device_id_type=MESH
        )

    @pl.when(col > 0)
    def _():
        pl.semaphore_signal(barrier, inc=1, device_id={"ctx": me - 2}, device_id_type=MESH)

    @pl.when(col < columns - 1)
    def _():
        pl.semaphore_signal(barrier, inc=1, device_id={"ctx": me + 2}, device_id_type=MESH)

    def remote(src, dst, ssem, rsem, device):
        return pltpu.make_async_remote_copy(
            src_ref=src,
            dst_ref=dst,
            send_sem=ssem,
            recv_sem=rsem,
            device_id=device,
            device_id_type=MESH,
        )

    def x0_copy(q):
        return remote(s_buf.at[q], rx0.at[q], x0_s.at[q], x0_r.at[q], {"ctx": partner})

    def up_copy(k, q):
        return remote(
            up.at[q], rc.at[k - 1, q], up_s.at[q], rc_r.at[k - 1, q], {"ctx": me + 2}
        )

    def forward_copy(k, q):
        return remote(
            rc.at[k - 1, q],
            rc.at[k - 1, q],
            fw_s.at[k - 1, q],
            rc_r.at[k - 1, q],
            {"ctx": me + 2},
        )

    def back_copy(k, q):
        return remote(
            g_buf.at[k, q],
            rb.at[k - 1, q],
            bk_s.at[k - 1, q],
            rb_r.at[k - 1, q],
            {"ctx": me - 2},
        )

    def xb_copy(q):
        return remote(xb.at[q], rxb.at[q], xb_s.at[q], xb_r.at[q], {"ctx": partner})

    hot = (
        lax.broadcasted_iota(jnp.int32, (table_ref.shape[0], toks), 0) == index_ref[...]
    ).astype(F32)
    w_t = lax.dot_general(
        table_ref[...],
        hot,
        (((0,), (0,)), ((), ())),
        preferred_element_type=F32,
        precision=lax.Precision.HIGHEST,
    )
    w_ref[...] = w_t.T
    b_t = b_ref[...].astype(F32).T.astype(BF16)
    c_f = c_ref[...].astype(F32)
    c_t = c_f.T
    for k in range(bits):
        lam_t = w_t[low_bits + 1 + k : low_bits + 2 + k, :]
        rise_t[k * nstate : (k + 1) * nstate, :] = (c_t * lam_t).astype(BF16)

    ends = (col > 0).astype(jnp.int32) + (col < columns - 1).astype(jnp.int32)
    pl.semaphore_wait(barrier, 1 + head_bits + ends)

    for q in range(chunks):
        cols = slice(q * WIDTH, (q + 1) * WIDTH)
        fill(x_hbm, x_ref, 0, q).wait()
        s_buf[q] = mm(b_t, x_ref[:, cols])
        x0_copy(q).start()
    for q in range(chunks):
        cols = slice(q * WIDTH, (q + 1) * WIDTH)
        fill(d_hbm, d_ref, 1, q).wait()
        g_buf[:, q] = mm(rise_t[...], d_ref[:, cols]).reshape(bits, nstate, WIDTH)
        if bits > 1:

            @pl.when(ready[bits - 1])
            def _():
                back_copy(bits - 1, q).start()

    for k in reversed(range(1, bits - 1)):
        for q in range(chunks):

            @pl.when(ready[k])
            def _():
                back_copy(k, q).start()

    def tile(i, j):
        rows = slice(i * TILE, (i + 1) * TILE)
        cols = slice(j * TILE, (j + 1) * TILE)
        w_rows = w_ref[rows, :]
        if i == j:
            row = lax.broadcasted_iota(jnp.int32, (TILE, TILE), 0)
            at = lax.broadcasted_iota(jnp.int32, (TILE, TILE), 1)
            level = bit_count(row ^ at, tile_bits)
            weight = jnp.zeros((TILE, TILE), F32)
            for n in range(tile_bits + 1):
                weight = jnp.where(level == n, w_rows[:, n : n + 1], weight)
            weight = jnp.where(at <= row, weight, 0.0)
        else:
            level = tile_bits + (i ^ j).bit_length()
            weight = w_rows[:, level : level + 1]
        x_j, d_i, b_j, c_i = x_ref[cols, :], d_ref[rows, :], b_ref[cols, :], c_ref[rows, :]
        mix = (mm_nt(c_i, b_j) * weight).astype(BF16)
        d_mix = (mm_nt(d_i, x_j) * weight).astype(BF16)
        y_t, dx_t = mm(mix, x_j), mm_tn(mix, d_i)
        dc_t, db_t = mm(d_mix, b_j), mm_tn(d_mix, c_i)
        if i == j:
            y_acc[rows, :] = y_t
            dx_acc[cols, :] = dx_t
            grads[1, rows, :] = dc_t
            grads[0, cols, :] = db_t
        else:
            y_acc[rows, :] += y_t
            dx_acc[cols, :] += dx_t
            grads[1, rows, :] += dc_t
            grads[0, cols, :] += db_t

    def pass_up(q):
        x0_copy(q).wait_recv()
        for k in levels:

            @pl.when(low_top[k])
            def _():
                group = s_buf[q] + rx0[q]
                for j in range(1, k):
                    up_copy(j, q).wait_recv()
                    group = group + rc[j - 1, q]
                up[q] = group
                up_copy(k, q).start()

    def relay_up(q):
        for k in levels:

            @pl.when(relay[k])
            def _():
                up_copy(k, q).wait_recv()
                forward_copy(k, q).start()

    def relay_down(q):
        for k in reversed(levels):

            @pl.when(relay[k])
            def _():
                back_copy(k, q).wait_recv()
                g_buf[k, q] = g_buf[k, q] + rb[k - 1, q]
                back_copy(k, q).start()

    def pass_down(q):
        @pl.when(last)
        def _():
            tot[q] = jnp.zeros_like(tot[q])

        for k in levels:

            @pl.when(low_top[k])
            def _():
                back_copy(k, q).wait_recv()
                got = rb[k - 1, q]
                tot[q] = got
                for j in range(1, k):
                    g_buf[j, q] = g_buf[j, q] + got
                    back_copy(j, q).start()

        @pl.when(par == 1)
        def _():
            xb[q] = tot[q] + g_buf[0, q]

        @pl.when(par == 0)
        def _():
            xb[q] = tot[q]

        xb_copy(q).start()

    def far_up(q):
        cols = slice(q * WIDTH, (q + 1) * WIDTH)
        for k in range(bits):
            at = slice(k * nstate, (k + 1) * nstate)
            if k:

                @pl.when(late[k])
                def _():
                    up_copy(k, q).wait_recv()

            @pl.when(is_set[k])
            def _():
                carry[at, :] = (rc[k - 1, q] if k else rx0[q]).astype(BF16)

            @pl.when(jnp.logical_not(is_set[k]))
            def _():
                carry[at, :] = jnp.zeros((nstate, WIDTH), BF16)

        y_ref[:, cols] = (y_acc[:, cols] + mm(rise[...], carry[...])).astype(BF16)
        for i in range(blocks):
            rows = slice(i * TILE, (i + 1) * TILE)
            terms = mm_nt(d_ref[rows, cols], carry[...])
            total = grads[1, rows, :]
            for k in range(bits):
                lam = w_ref[rows, low_bits + 1 + k : low_bits + 2 + k]
                total = total + terms[:, k * nstate : (k + 1) * nstate] * lam
            grads[1, rows, :] = total

    def far_down(q):
        cols = slice(q * WIDTH, (q + 1) * WIDTH)
        xb_copy(q).wait_recv()
        back = (tot[q] + rxb[q]).astype(BF16)
        dx_ref[:, cols] = (dx_acc[:, cols] + mm(b_ref[...], back)).astype(BF16)
        grads[0] = grads[0] + mm_nt(x_ref[:, cols], back)

    part = toks // heads
    waits = []

    def piece(array, digit, g, which):
        if digit == 0:
            start = pl.multiple_of((2 * g + which) * part, part)
            return grads.at[array, pl.ds(start, part)]
        return r_out[digit - 1].at[array, 2 * g + which]

    def halve_start(array, digit):
        mine = (head // (1 << digit)) % 2
        peer = head + (1 - 2 * mine) * (1 << digit)
        copies = []
        for g in range(heads >> (digit + 1)):
            copies.append(
                remote(
                    piece(array, digit, g, 1 - mine),
                    r_in[digit].at[array, g],
                    hd_sems[2 * digit].at[array, g],
                    hd_sems[2 * digit + 1].at[array, g],
                    {"head": peer},
                )
            )
            copies[-1].start()
        waits.extend(copies)
        return copies

    def halve_end(array, digit, copies):
        mine = (head // (1 << digit)) % 2
        for g, copy in enumerate(copies):
            copy.wait_recv()
            value = piece(array, digit, g, mine)[...] + r_in[digit][array, g]
            if digit < head_bits - 1:
                r_out[digit][array, g] = value
            else:
                (db_ref, dc_ref)[array][...] = value

    tiles = [(i, i) for i in range(blocks)]
    tiles += [(i, j) for i in range(blocks) for j in range(i)]

    def near(amount):
        for _ in range(min(amount, len(tiles))):
            tile(*tiles.pop(0))

    def pass_down_if(condition, q):
        @pl.when(condition)
        def _():
            pass_down(q)

    slow = low_top[1] if bits > 1 else col < 0
    quick = jnp.logical_not(slow)
    for n in range(chunks + 2):
        if n < chunks:
            pass_up(n)
        if 0 < n <= chunks:
            relay_down(n - 1)
        if n > 1:
            pass_down_if(quick, n - 2)
        near(1)
    for k in range(bits):
        lam = w_ref[:, low_bits + 1 + k : low_bits + 2 + k]
        rise[:, k * nstate : (k + 1) * nstate] = (c_f * lam).astype(BF16)
    for n in range(chunks + 1):
        if n < chunks:
            relay_up(n)
        near(1)
        if n:
            pass_down_if(slow, n - 1)
    near(len(tiles))
    for n in range(chunks):
        far_up(n)
    jobs = halve_start(1, 0) if head_bits else []
    for n in range(chunks):
        far_down(n)
    jobs_b = halve_start(0, 0) if head_bits else []
    for digit in range(head_bits):
        halve_end(1, digit, jobs)
        if digit < head_bits - 1:
            jobs = halve_start(1, digit + 1)
        halve_end(0, digit, jobs_b)
        if digit < head_bits - 1:
            jobs_b = halve_start(0, digit + 1)
    if not head_bits:
        db_ref[...] = grads[0]
        dc_ref[...] = grads[1]

    for copy in waits:
        copy.wait_send()
    for q in range(chunks):
        x0_copy(q).wait_send()
        xb_copy(q).wait_send()
        for k in levels:

            @pl.when(low_top[k])
            def _():
                up_copy(k, q).wait_send()

            @pl.when(relay[k])
            def _():
                forward_copy(k, q).wait_send()

            @pl.when(is_set[k])
            def _():
                back_copy(k, q).wait_send()


def local(x_in, b_in, c_in, d_out, table, level_index):
    toks, feats = x_in.shape
    nstate = b_in.shape[1]
    count, heads = lax.axis_size("ctx"), lax.axis_size("head")
    bits, head_bits = count.bit_length() - 1, heads.bit_length() - 1
    chunks = feats // WIDTH
    table = jnp.pad(table, ((0, 0), (0, nstate - table.shape[1])))
    index = level_index.reshape(1, toks)
    rows = toks // heads
    ups = max(bits - 1, 1)
    vmem = pl.BlockSpec(memory_space=pltpu.VMEM)
    hbm = pl.BlockSpec(memory_space=pl.ANY)
    dma = pltpu.SemaphoreType.DMA
    slab = (chunks, nstate, WIDTH)
    halves = [heads >> (n + 1) for n in range(head_bits)]
    return pl.pallas_call(
        functools.partial(kernel, count, heads),
        out_shape=(
            pltpu.VMEM((toks, feats), BF16),
            pltpu.VMEM((toks, feats), BF16),
            pltpu.VMEM((rows, nstate), F32),
            pltpu.VMEM((rows, nstate), F32),
        ),
        in_specs=[hbm, vmem, vmem, hbm, vmem, vmem],
        out_specs=(vmem,) * 4,
        scratch_shapes=[
            pltpu.VMEM((toks, feats), BF16),
            pltpu.VMEM((toks, feats), BF16),
            pltpu.VMEM((toks, nstate), F32),
            pltpu.VMEM((toks, feats), F32),
            pltpu.VMEM((toks, feats), F32),
            pltpu.VMEM((2, toks, nstate), F32),
            pltpu.VMEM((toks, bits * nstate), BF16),
            pltpu.VMEM((bits * nstate, toks), BF16),
            pltpu.VMEM((bits * nstate, WIDTH), BF16),
            pltpu.VMEM(slab, F32),
            pltpu.VMEM((bits,) + slab, F32),
            pltpu.VMEM(slab, F32),
            pltpu.VMEM(slab, F32),
            pltpu.VMEM((ups,) + slab, F32),
            pltpu.VMEM((ups,) + slab, F32),
            pltpu.VMEM(slab, F32),
            pltpu.VMEM(slab, F32),
            pltpu.VMEM(slab, F32),
        ]
        + [pltpu.VMEM((2, half, rows, nstate), F32) for half in halves]
        + [pltpu.VMEM((2, half, rows, nstate), F32) for half in halves[:-1]]
        + [
            dma((2, chunks)),
            dma((chunks,)),
            dma((chunks,)),
            dma((chunks,)),
            dma((ups, chunks)),
            dma((ups, chunks)),
            dma((ups, chunks)),
            dma((ups, chunks)),
            dma((chunks,)),
            dma((chunks,)),
        ]
        + [dma((2, half)) for half in halves for _ in range(2)],
        compiler_params=pltpu.CompilerParams(
            collective_id=0, has_side_effects=True, vmem_limit_bytes=48 * 1024 * 1024
        ),
    )(x_in, b_in, c_in, d_out, table, index)


def solution(mesh):
    return jax.shard_map(
        local,
        mesh=mesh,
        in_specs=(
            P("ctx", "head"),
            P("ctx", None),
            P("ctx", None),
            P("ctx", "head"),
            P(),
            P("ctx"),
        ),
        out_specs=(
            P("ctx", "head"),
            P("ctx", "head"),
            P(("ctx", "head"), None),
            P(("ctx", "head"), None),
        ),
        check_vma=False,
    )
```

```python
import functools

import jax
import jax.numpy as jnp
from jax import lax
from jax.experimental import pallas as pl
from jax.experimental.pallas import tpu as pltpu
from jax.sharding import PartitionSpec as P

F32 = jnp.float32
BF16 = jnp.bfloat16
MESH = pl.DeviceIdType.MESH
TILE = 256
WIDTH = 256
VMEM_BYTES = 67043328
SPARE = 16384


def mm(a, b):
    return jnp.dot(a, b, preferred_element_type=F32)


def mm_tn(a, b):
    return lax.dot_general(a, b, (((0,), (0,)), ((), ())), preferred_element_type=F32)


def mm_nt(a, b):
    return lax.dot_general(a, b, (((1,), (1,)), ((), ())), preferred_element_type=F32)


def bit_count(values, bits):
    counted = jnp.zeros(values.shape, jnp.int32)
    for digit_no in range(bits):
        counted = counted + (values >= 1 << digit_no).astype(jnp.int32)
    return counted


def kernel(
    count,
    heads,
    x_hbm,
    b_hbm,
    c_hbm,
    d_hbm,
    table_hbm,
    index_hbm,
    y_ref,
    dx_ref,
    db_ref,
    dc_ref,
    x_ref,
    d_ref,
    b_ref,
    c_ref,
    table_ref,
    index_ref,
    wide_table,
    w_ref,
    y_acc,
    dx_acc,
    grads,
    rise,
    rise_t,
    carry,
    s_buf,
    g_buf,
    rx0,
    up,
    rc,
    rb,
    tot,
    xb,
    rxb,
    *rest,
):
    bits = count.bit_length() - 1
    head_bits = heads.bit_length() - 1
    r_in = rest[:head_bits]
    r_out = rest[head_bits : 2 * head_bits - 1]
    sems = rest[2 * head_bits - 1 :]
    small_sem, in_sem, x0_s, x0_r, up_s, fw_s, rc_r, bk_s, rb_r, xb_s, xb_r = sems[:11]
    hd_sems = sems[11:]
    toks, feats = x_ref.shape
    nstate = b_ref.shape[1]
    chunks = feats // WIDTH
    blocks = toks // TILE
    tile_bits = TILE.bit_length() - 1
    low_bits = toks.bit_length() - 1
    me = lax.axis_index("ctx")
    head = lax.axis_index("head")
    par = me % 2
    col = me // 2
    levels = range(1, bits)
    columns = count // 2
    is_set = {k: (me // (1 << k)) % 2 == 1 for k in range(bits)}
    low_top = {k: col % (1 << k) == (1 << (k - 1)) - 1 for k in levels}
    up_top = {k: col % (1 << k) == (1 << k) - 1 for k in levels}
    relay = {k: is_set[k] & jnp.logical_not(up_top[k]) for k in levels}
    last = col == columns - 1
    ready = {k: up_top[k] & last for k in levels}
    early = {k: up_top[k] & jnp.logical_not(last) for k in levels}
    late = {k: up_top[k] & last for k in levels}

    def fill(hbm, vmem, n, q):
        cols = pl.ds(q * WIDTH, WIDTH)
        return pltpu.make_async_copy(hbm.at[:, cols], vmem.at[:, cols], in_sem.at[n, q])

    smalls = [
        pltpu.make_async_copy(hbm, vmem, small_sem.at[n])
        for n, (hbm, vmem) in enumerate(
            (
                (b_hbm, b_ref),
                (c_hbm, c_ref),
                (table_hbm, table_ref),
                (index_hbm, index_ref),
            )
        )
    ]
    smalls[0].start()
    for q in range(chunks):
        fill(x_hbm, x_ref, 0, q).start()
    for small in smalls[1:]:
        small.start()
    for q in range(chunks):
        fill(d_hbm, d_ref, 1, q).start()

    partner = me + 1 - 2 * par
    barrier = pltpu.get_barrier_semaphore()
    pl.semaphore_signal(barrier, inc=1, device_id={"ctx": partner}, device_id_type=MESH)
    for digit in range(head_bits):
        flip = 1 - 2 * ((head // (1 << digit)) % 2)
        pl.semaphore_signal(
            barrier, inc=1, device_id={"head": head + flip * (1 << digit)}, device_id_type=MESH
        )

    @pl.when(col > 0)
    def _():
        pl.semaphore_signal(barrier, inc=1, device_id={"ctx": me - 2}, device_id_type=MESH)

    @pl.when(col < columns - 1)
    def _():
        pl.semaphore_signal(barrier, inc=1, device_id={"ctx": me + 2}, device_id_type=MESH)

    def remote(src, dst, ssem, rsem, device):
        return pltpu.make_async_remote_copy(
            src_ref=src,
            dst_ref=dst,
            send_sem=ssem,
            recv_sem=rsem,
            device_id=device,
            device_id_type=MESH,
        )

    def x0_copy(q):
        return remote(s_buf.at[q], rx0.at[q], x0_s.at[q], x0_r.at[q], {"ctx": partner})

    def up_copy(k, q):
        return remote(
            up.at[q], rc.at[k - 1, q], up_s.at[q], rc_r.at[k - 1, q], {"ctx": me + 2}
        )

    def forward_copy(k, q):
        return remote(
            rc.at[k - 1, q],
            rc.at[k - 1, q],
            fw_s.at[k - 1, q],
            rc_r.at[k - 1, q],
            {"ctx": me + 2},
        )

    def back_copy(k, q):
        return remote(
            g_buf.at[k, q],
            rb.at[k - 1, q],
            bk_s.at[k - 1, q],
            rb_r.at[k - 1, q],
            {"ctx": me - 2},
        )

    def xb_copy(q):
        return remote(xb.at[q], rxb.at[q], xb_s.at[q], xb_r.at[q], {"ctx": partner})

    smalls[0].wait()
    b_t = b_ref[...].astype(F32).T.astype(BF16)
    ends = (col > 0).astype(jnp.int32) + (col < columns - 1).astype(jnp.int32)
    pl.semaphore_wait(barrier, 1 + head_bits + ends)

    for q in range(chunks):
        cols = slice(q * WIDTH, (q + 1) * WIDTH)
        fill(x_hbm, x_ref, 0, q).wait()
        s_buf[q] = mm(b_t, x_ref[:, cols])
        x0_copy(q).start()

    for small in smalls[1:]:
        small.wait()
    wide_table[...] = jnp.zeros_like(wide_table)
    wide_table[:, : table_ref.shape[1]] = table_ref[...]
    hot = (
        lax.broadcasted_iota(jnp.int32, (table_ref.shape[0], toks), 0) == index_ref[...]
    ).astype(F32)
    w_t = lax.dot_general(
        wide_table[...],
        hot,
        (((0,), (0,)), ((), ())),
        preferred_element_type=F32,
        precision=lax.Precision.HIGHEST,
    )
    w_ref[...] = w_t.T
    c_f = c_ref[...].astype(F32)
    c_t = c_f.T
    for k in range(bits):
        lam_t = w_t[low_bits + 1 + k : low_bits + 2 + k, :]
        rise_t[k * nstate : (k + 1) * nstate, :] = (c_t * lam_t).astype(BF16)

    for q in range(chunks):
        cols = slice(q * WIDTH, (q + 1) * WIDTH)
        fill(d_hbm, d_ref, 1, q).wait()
        g_buf[:, q] = mm(rise_t[...], d_ref[:, cols]).reshape(bits, nstate, WIDTH)
        if bits > 1:

            @pl.when(ready[bits - 1])
            def _():
                back_copy(bits - 1, q).start()

    for k in reversed(range(1, bits - 1)):
        for q in range(chunks):

            @pl.when(ready[k])
            def _():
                back_copy(k, q).start()

    def tile(i, j):
        rows = slice(i * TILE, (i + 1) * TILE)
        cols = slice(j * TILE, (j + 1) * TILE)
        w_rows = w_ref[rows, :]
        if i == j:
            row = lax.broadcasted_iota(jnp.int32, (TILE, TILE), 0)
            at = lax.broadcasted_iota(jnp.int32, (TILE, TILE), 1)
            level = bit_count(row ^ at, tile_bits)
            weight = jnp.zeros((TILE, TILE), F32)
            for n in range(tile_bits + 1):
                weight = jnp.where(level == n, w_rows[:, n : n + 1], weight)
            weight = jnp.where(at <= row, weight, 0.0)
        else:
            level = tile_bits + (i ^ j).bit_length()
            weight = w_rows[:, level : level + 1]
        x_j, d_i, b_j, c_i = x_ref[cols, :], d_ref[rows, :], b_ref[cols, :], c_ref[rows, :]
        mix = (mm_nt(c_i, b_j) * weight).astype(BF16)
        d_mix = (mm_nt(d_i, x_j) * weight).astype(BF16)
        y_t, dx_t = mm(mix, x_j), mm_tn(mix, d_i)
        dc_t, db_t = mm(d_mix, b_j), mm_tn(d_mix, c_i)
        if i == j:
            y_acc[rows, :] = y_t
            dx_acc[cols, :] = dx_t
            grads[1, rows, :] = dc_t
            grads[0, cols, :] = db_t
        else:
            y_acc[rows, :] += y_t
            dx_acc[cols, :] += dx_t
            grads[1, rows, :] += dc_t
            grads[0, cols, :] += db_t

    def pass_up(q):
        x0_copy(q).wait_recv()
        for k in levels:

            @pl.when(low_top[k])
            def _():
                group = s_buf[q] + rx0[q]
                for j in range(1, k):
                    up_copy(j, q).wait_recv()
                    group = group + rc[j - 1, q]
                up[q] = group
                up_copy(k, q).start()

    def relay_up(q):
        for k in levels:

            @pl.when(relay[k])
            def _():
                up_copy(k, q).wait_recv()
                forward_copy(k, q).start()

    def relay_down(q):
        for k in reversed(levels):

            @pl.when(relay[k])
            def _():
                back_copy(k, q).wait_recv()
                g_buf[k, q] = g_buf[k, q] + rb[k - 1, q]
                back_copy(k, q).start()

    def pass_down(q):
        @pl.when(last)
        def _():
            tot[q] = jnp.zeros_like(tot[q])

        for k in levels:

            @pl.when(low_top[k])
            def _():
                back_copy(k, q).wait_recv()
                got = rb[k - 1, q]
                tot[q] = got
                for j in range(1, k):
                    g_buf[j, q] = g_buf[j, q] + got
                    back_copy(j, q).start()

        @pl.when(par == 1)
        def _():
            xb[q] = tot[q] + g_buf[0, q]

        @pl.when(par == 0)
        def _():
            xb[q] = tot[q]

        xb_copy(q).start()

    def far_up(q):
        cols = slice(q * WIDTH, (q + 1) * WIDTH)
        for k in range(bits):
            at = slice(k * nstate, (k + 1) * nstate)
            if k:

                @pl.when(late[k])
                def _():
                    up_copy(k, q).wait_recv()

            @pl.when(is_set[k])
            def _():
                carry[at, :] = (rc[k - 1, q] if k else rx0[q]).astype(BF16)

            @pl.when(jnp.logical_not(is_set[k]))
            def _():
                carry[at, :] = jnp.zeros((nstate, WIDTH), BF16)

        y_ref[:, cols] = (y_acc[:, cols] + mm(rise[...], carry[...])).astype(BF16)
        for i in range(blocks):
            rows = slice(i * TILE, (i + 1) * TILE)
            terms = mm_nt(d_ref[rows, cols], carry[...])
            total = grads[1, rows, :]
            for k in range(bits):
                lam = w_ref[rows, low_bits + 1 + k : low_bits + 2 + k]
                total = total + terms[:, k * nstate : (k + 1) * nstate] * lam
            grads[1, rows, :] = total

    def far_down(q):
        cols = slice(q * WIDTH, (q + 1) * WIDTH)
        xb_copy(q).wait_recv()
        back = (tot[q] + rxb[q]).astype(BF16)
        dx_ref[:, cols] = (dx_acc[:, cols] + mm(b_ref[...], back)).astype(BF16)
        grads[0] = grads[0] + mm_nt(x_ref[:, cols], back)

    part = toks // heads
    waits = []

    def piece(array, digit, g, which):
        if digit == 0:
            start = pl.multiple_of((2 * g + which) * part, part)
            return grads.at[array, pl.ds(start, part)]
        return r_out[digit - 1].at[array, 2 * g + which]

    def halve_start(array, digit):
        mine = (head // (1 << digit)) % 2
        peer = head + (1 - 2 * mine) * (1 << digit)
        copies = []
        for g in range(heads >> (digit + 1)):
            copies.append(
                remote(
                    piece(array, digit, g, 1 - mine),
                    r_in[digit].at[array, g],
                    hd_sems[2 * digit].at[array, g],
                    hd_sems[2 * digit + 1].at[array, g],
                    {"head": peer},
                )
            )
            copies[-1].start()
        waits.extend(copies)
        return copies

    def halve_end(array, digit, copies):
        mine = (head // (1 << digit)) % 2
        for g, copy in enumerate(copies):
            copy.wait_recv()
            value = piece(array, digit, g, mine)[...] + r_in[digit][array, g]
            if digit < head_bits - 1:
                r_out[digit][array, g] = value
            else:
                (db_ref, dc_ref)[array][...] = value

    tiles = [(i, i) for i in range(blocks)]
    tiles += [(i, j) for i in range(blocks) for j in range(i)]

    def near(amount):
        for _ in range(min(amount, len(tiles))):
            tile(*tiles.pop(0))

    def pass_down_if(condition, q):
        @pl.when(condition)
        def _():
            pass_down(q)

    slow = low_top[1] if bits > 1 else col < 0
    quick = jnp.logical_not(slow)
    slots = chunks + 2
    for n in range(slots):
        if n < chunks:
            pass_up(n)
        if 0 < n <= chunks:
            relay_down(n - 1)
        if n > 1:
            pass_down_if(quick, n - 2)
        near(pl.cdiv(len(tiles), slots - n))
    for k in range(bits):
        lam = w_ref[:, low_bits + 1 + k : low_bits + 2 + k]
        rise[:, k * nstate : (k + 1) * nstate] = (c_f * lam).astype(BF16)
    for n in range(chunks + 1):
        if n < chunks:
            relay_up(n)
        if n:
            pass_down_if(slow, n - 1)
        if n < chunks:
            far_up(n)
    jobs = halve_start(1, 0) if head_bits else []
    for n in range(chunks):
        far_down(n)
        if n == max(chunks // 2 - 1, 0) and head_bits:
            halve_end(1, 0, jobs)
            jobs = halve_start(1, 1) if head_bits > 1 else []
    for digit in range(head_bits):
        jobs_b = halve_start(0, digit)
        if digit:
            halve_end(1, digit, jobs)
            jobs = halve_start(1, digit + 1) if digit < head_bits - 1 else []
        halve_end(0, digit, jobs_b)
    if not head_bits:
        db_ref[...] = grads[0]
        dc_ref[...] = grads[1]

    for copy in waits:
        copy.wait_send()
    for q in range(chunks):
        x0_copy(q).wait_send()
        xb_copy(q).wait_send()
        for k in levels:

            @pl.when(low_top[k])
            def _():
                up_copy(k, q).wait_send()

            @pl.when(relay[k])
            def _():
                forward_copy(k, q).wait_send()

            @pl.when(is_set[k])
            def _():
                back_copy(k, q).wait_send()


def write_out(*refs):
    copies = [pltpu.make_async_copy(refs[n], refs[n + 4], refs[8].at[n]) for n in range(4)]
    for copy in copies:
        copy.start()
    for copy in copies:
        copy.wait()


def local(x_in, b_in, c_in, d_out, table, level_index):
    toks, feats = x_in.shape
    nstate = b_in.shape[1]
    count, heads = lax.axis_size("ctx"), lax.axis_size("head")
    bits, head_bits = count.bit_length() - 1, heads.bit_length() - 1
    chunks = feats // WIDTH
    index = level_index.reshape(1, toks)
    rows = toks // heads
    ups = max(bits - 1, 1)
    vmem = pl.BlockSpec(memory_space=pltpu.VMEM)
    hbm = pl.BlockSpec(memory_space=pltpu.HBM)
    dma = pltpu.SemaphoreType.DMA
    slab = (chunks, nstate, WIDTH)
    halves = [heads >> (n + 1) for n in range(head_bits)]
    results = pl.pallas_call(
        functools.partial(kernel, count, heads),
        out_shape=(
            pltpu.VMEM((toks, feats), BF16),
            pltpu.VMEM((toks, feats), BF16),
            pltpu.VMEM((rows, nstate), F32),
            pltpu.VMEM((rows, nstate), F32),
        ),
        in_specs=[hbm] * 6,
        out_specs=(vmem,) * 4,
        scratch_shapes=[
            pltpu.VMEM((toks, feats), BF16),
            pltpu.VMEM((toks, feats), BF16),
            pltpu.VMEM((toks, nstate), BF16),
            pltpu.VMEM((toks, nstate), BF16),
            pltpu.VMEM(table.shape, F32),
            pltpu.VMEM((1, toks), jnp.int32),
            pltpu.VMEM((table.shape[0], nstate), F32),
            pltpu.VMEM((toks, nstate), F32),
            pltpu.VMEM((toks, feats), F32),
            pltpu.VMEM((toks, feats), F32),
            pltpu.VMEM((2, toks, nstate), F32),
            pltpu.VMEM((toks, bits * nstate), BF16),
            pltpu.VMEM((bits * nstate, toks), BF16),
            pltpu.VMEM((bits * nstate, WIDTH), BF16),
            pltpu.VMEM(slab, F32),
            pltpu.VMEM((bits,) + slab, F32),
            pltpu.VMEM(slab, F32),
            pltpu.VMEM(slab, F32),
            pltpu.VMEM((ups,) + slab, F32),
            pltpu.VMEM((ups,) + slab, F32),
            pltpu.VMEM(slab, F32),
            pltpu.VMEM(slab, F32),
            pltpu.VMEM(slab, F32),
        ]
        + [pltpu.VMEM((2, half, rows, nstate), F32) for half in halves]
        + [pltpu.VMEM((2, half, rows, nstate), F32) for half in halves[:-1]]
        + [
            dma((4,)),
            dma((2, chunks)),
            dma((chunks,)),
            dma((chunks,)),
            dma((chunks,)),
            dma((ups, chunks)),
            dma((ups, chunks)),
            dma((ups, chunks)),
            dma((ups, chunks)),
            dma((chunks,)),
            dma((chunks,)),
        ]
        + [dma((2, half)) for half in halves for _ in range(2)],
        compiler_params=pltpu.CompilerParams(
            collective_id=0, has_side_effects=True, vmem_limit_bytes=VMEM_BYTES - 4 * toks * feats - 8 * rows * nstate - SPARE
        ),
    )(x_in, b_in, c_in, d_out, table, index)
    return pl.pallas_call(
        write_out,
        out_shape=tuple(jax.ShapeDtypeStruct(r.shape, r.dtype) for r in results),
        in_specs=[vmem] * 4,
        out_specs=(hbm,) * 4,
        scratch_shapes=[dma((4,))],
        compiler_params=pltpu.CompilerParams(vmem_limit_bytes=1024 * 1024),
    )(*results)


def solution(mesh):
    return jax.shard_map(
        local,
        mesh=mesh,
        in_specs=(
            P("ctx", "head"),
            P("ctx", None),
            P("ctx", None),
            P("ctx", "head"),
            P(),
            P("ctx"),
        ),
        out_specs=(
            P("ctx", "head"),
            P("ctx", "head"),
            P(("ctx", "head"), None),
            P(("ctx", "head"), None),
        ),
        check_vma=False,
    )
```
